32 devices in a mesh: groups: 2 (over x), row: 8 (over z, y), col: 2 (over core).
Axes of the slice: x: 2, y: 2, z: 4, core: 2. Of those that a mesh axis runs over, the one named last changes fastest.
Arguments:
- queries: bfloat16 [8192, 1024], P(('groups', 'row', 'col')), parts along dimension 0, may hold values from -200 to 200
- keys: bfloat16 [8192, 128], P(('groups', 'row', 'col')), parts along dimension 0, may hold values from -5 to 5
- values: bfloat16 [8192, 128], P(('groups', 'row', 'col')), parts along dimension 0, may hold values from -6 to 6
- doc_lengths: int32 [32], P('groups'), parts along dimension 0, may hold values from 1 to 3072, 4096 in all
Outputs:
- attended: bfloat16 [8192, 1024], P(('groups', 'row', 'col')), parts along dimension 0
The draws below stay inside these ranges and needn't reach their ends.
There are 2 independent parts, one for each index of `groups`. The reference program is written for one: setup_inputs(seed, part) draws one part's arguments, and reference() takes and returns one part's arrays. A program takes and returns all parts, laid end to end along the dimension named above; each array names one. Nothing has to cross between parts.
Inputs may be any that keep to these rules, and one draw needn't show every extreme that they name: `doc_lengths`: the 16 lengths sum to 4096 and the longest is exactly 3072.
All inputs are finite; a program needn't handle non-finite values.
Results may differ from the reference program's by a relative error of at most 0.0055.
Values may be sent and summed in bfloat16 or wider, within the bound.
A program may use at most 64 MiB of HBM per device.

```python
import math
import jax
import jax.numpy as jnp
import numpy as np
from jax import lax

HEADS = 8
HEAD_DIM = 128
DOCS = 16
SEQ = 4096
MAXDOC = 3072


def shared_pair(key):
    key_keys = jax.random.fold_in(key, 12)
    key_queries = jax.random.fold_in(key, 11)
    keymat = jnp.clip(jax.random.normal(key_keys, (SEQ, HEAD_DIM), jnp.float32), -4.0, 4.0)
    querymat = jnp.clip(jax.random.normal(key_queries, (SEQ, HEADS, HEAD_DIM), jnp.float32), -4.0, 4.0)
    places = jnp.arange(SEQ)
    half_back = jnp.roll(keymat, SEQ // 2, axis=0)
    picked = (places % 61 == 30) & (places >= SEQ // 2)
    querymat = jnp.where(picked[:, None, None], half_back[:, None, :] + 0.0 * querymat, querymat)
    return (querymat, keymat)


def draw_queries(key, part):
    querymat, keymat = shared_pair(key)
    return querymat.reshape(SEQ, HEADS * HEAD_DIM).astype(jnp.bfloat16)


def draw_keys(key, part):
    querymat, keymat = shared_pair(key)
    return keymat.astype(jnp.bfloat16)


def block_scale(own_key, extent, pieces, least, top_value):
    loudness, own = 1.0, jax.random.fold_in(own_key, 6)
    for dim, parts in pieces:
        steps = jnp.exp(jax.random.uniform(jax.random.fold_in(own, dim), (parts,), jnp.float32, least / len(pieces), top_value / len(pieces)))
        loudness = loudness * jnp.repeat(steps, extent[dim] // parts).reshape([-1 if axis == dim else 1 for axis in range(len(extent))])
    return loudness


def length_profile(number_of, total, reach, slope):
    loads = [(1 << 20) // math.isqrt(standing ** slope) + 1 for standing in range(2, number_of + 1)]
    spare, holding = total - reach - (number_of - 1), [1] * (number_of - 1)
    while spare > 0:
        candidates = [i for i in range(number_of - 1) if holding[i] < reach]
        mass, left = sum([loads[i] for i in candidates]), spare
        for i in candidates:
            addition = min(reach - holding[i], max(1, left * loads[i] // mass), spare)
            holding[i] = holding[i] + addition
            spare = spare - addition
    return np.array([reach] + holding)


def uneven(own_key, amount, total, limit, lean):
    if amount == 2:
        one = jax.random.randint(own_key, (), max(1, total - limit), min(limit, total - 1) + 1)
        return jnp.stack([one, total - one])
    tallies = jnp.asarray(length_profile(amount, total, limit, lean), jnp.int32)
    twos = (amount - 1) // 2
    donor, taker = tallies[1:1 + 2 * twos:2], tallies[2:2 + 2 * twos:2]
    margin = jnp.minimum(donor - 1, limit - taker)
    moved = jax.random.randint(jax.random.fold_in(own_key, 1), (twos,), 0, 1 << 20) % (margin + 1)
    tallies = tallies.at[1:1 + 2 * twos:2].set(donor - moved).at[2:2 + 2 * twos:2].set(taker + moved)
    return tallies[jax.random.permutation(jax.random.fold_in(own_key, 2), amount)]


def gaussian(stream_key, extent, width, most, split=(), kind=jnp.bfloat16):
    array = width * jax.random.normal(stream_key, extent, jnp.float32)
    if split:
        array = array * block_scale(stream_key, extent, split, -0.22, 0.18)
    return jnp.clip(array, -most, most).astype(kind)


def setup_inputs(seed: int = 0, part: int = 0) -> dict:
    key_of = jax.random.split(jax.random.key(seed), 5)
    part_splits = jax.random.split(jax.random.fold_in(key_of[4], part), 5)
    return {
        "queries": draw_queries(jax.random.fold_in(jax.random.fold_in(key_of[4], part), 71), part),
        "keys": draw_keys(jax.random.fold_in(jax.random.fold_in(key_of[4], part), 71), part),
        "values": gaussian(part_splits[2], (SEQ, HEAD_DIM), 1.0, 6.0, ((0, 16),)),
        "doc_lengths": uneven(part_splits[3], DOCS, SEQ, MAXDOC, 2).astype(jnp.int32),
    }


def reference(queries, keys, values, doc_lengths):
    ends = jnp.cumsum(doc_lengths).astype(jnp.int32)
    places = jnp.arange(SEQ, dtype=jnp.int32)
    owner = jnp.sum((places[:, None] >= ends[None, :]).astype(jnp.int32), axis=1)
    qmat = queries.reshape(SEQ, HEADS, HEAD_DIM).astype(jnp.float32)
    kmat = keys.astype(jnp.float32)
    value_matrix = values.astype(jnp.float32)
    block = math.gcd(SEQ, 512)
    scale = HEAD_DIM ** -0.5

    def one_block(index):
        first = (index * block).astype(jnp.int32)
        qpart = lax.dynamic_slice_in_dim(qmat, first, block, 0)
        qpos = first + jnp.arange(block, dtype=jnp.int32)
        qdoc = lax.dynamic_slice_in_dim(owner, first, block, 0)
        scores = jnp.einsum("qhd,kd->qhk", qpart, kmat, precision=lax.Precision.HIGHEST) * scale
        visible = (owner[None, :] == qdoc[:, None]) & (places[None, :] <= qpos[:, None])
        masked = jnp.where(visible[:, None, :], scores, jnp.float32(-1e30))
        top = jnp.max(masked, axis=-1)
        weights = jnp.where(visible[:, None, :], jnp.exp(scores - top[..., None]), jnp.float32(0.0))
        total = jnp.sum(weights, axis=-1)
        rounded_down_value = weights.astype(jnp.bfloat16).astype(jnp.float32)
        summed_values = jnp.einsum("uxa,ag->uxg", rounded_down_value, value_matrix, precision=lax.Precision.HIGHEST)
        return (summed_values / total[..., None]).astype(jnp.bfloat16)

    outcome = lax.map(one_block, jnp.arange(SEQ // block, dtype=jnp.int32))
    return outcome.reshape(SEQ, HEADS * HEAD_DIM)
```

```python
import functools

import jax
import jax.numpy as jnp
from jax import lax
from jax.experimental import pallas as pl
from jax.experimental.pallas import tpu as pltpu
from jax.sharding import PartitionSpec as P

HEAD_DIM = 128
RATE = HEAD_DIM ** (-0.5) * 1.4426950408889634
MASKED = -1e30
AHEAD_SLOTS = 8
SUM_ROWS = 16
PIECES = 2


def kernel(
    n_row,
    n_col,
    lanes,
    reach,
    lens_ref,
    q_hbm,
    k_hbm,
    v_hbm,
    o_ref,
    kv,
    q_ref,
    member_ref,
    top_ref,
    total_ref,
    acc_ref,
    s_ref,
    load_sem,
    in_sem,
    mate_sem,
    up_send,
    cross_send,
    mate_send,
):
    shard = q_hbm.shape[0]
    heads = q_hbm.shape[1] // HEAD_DIM
    levels = n_row // lanes
    tile = n_col * shard
    piece = 2 * shard // PIECES
    furthest = min(levels - 1, (reach + lanes - 1) // lanes)
    has_other = lanes > 1
    row = lax.axis_index("row")
    col = lax.axis_index("col")
    level = row // lanes
    lane = row % lanes
    mate = 1 - col
    other = level * lanes + (lanes - 1 - lane)
    has_up = level + 1 < levels
    has_down = level > 0

    def needs(reader, source):
        return (source >= 0) & (reader > source) & (reader - source <= reach)

    def straight(dist):
        return row - dist * lanes

    def crossed(dist):
        return other - dist * lanes

    barrier = pltpu.get_barrier_semaphore()
    pl.semaphore_signal(barrier, inc=1, device_id={"col": mate})
    if has_other:
        pl.semaphore_signal(barrier, inc=1, device_id={"row": other})

    @pl.when(has_up)
    def _():
        pl.semaphore_signal(barrier, inc=1, device_id={"row": row + lanes})

    @pl.when(has_down)
    def _():
        pl.semaphore_signal(barrier, inc=1, device_id={"row": row - lanes})

    load_k = pltpu.make_async_copy(k_hbm, kv.at[row, col, :shard, :], load_sem.at[0])
    load_v = pltpu.make_async_copy(v_hbm, kv.at[row, col, shard:, :], load_sem.at[1])
    load_q = pltpu.make_async_copy(q_hbm, q_ref, load_sem.at[2])
    for load in (load_k, load_v, load_q):
        load.start()

    def copy(source, rows, send_sem, recv_sem, device):
        here = kv.at[source, col, rows, :]
        return pltpu.make_async_remote_copy(
            src_ref=here,
            dst_ref=here,
            send_sem=send_sem,
            recv_sem=recv_sem,
            device_id=device,
            device_id_type=pl.DeviceIdType.MESH,
        )

    def part(p):
        return pl.ds(p * piece, piece)

    def to_up(source, p, dist):
        recv = in_sem.at[2 * dist + 2, p]
        return copy(source, part(p), up_send.at[dist], recv, {"row": row + lanes})

    def to_other(source, p, dist):
        recv = in_sem.at[2 * dist + 1, p]
        return copy(source, part(p), cross_send.at[dist], recv, {"row": other})

    def to_mate(source, unit):
        whole = pl.ds(0, 2 * shard)
        return copy(source, whole, mate_send.at[unit], mate_sem.at[unit], {"col": mate})

    def wait_whole(source, sem):
        here = kv.at[source, col, :, :]
        pltpu.make_async_copy(here, here, sem).wait()

    def wait_part(source, p, sem):
        here = kv.at[source, col, part(p), :]
        pltpu.make_async_copy(here, here, sem).wait()

    own_up = has_up
    own_cross = needs(other, row)
    own_mate = col < mate

    count = 1 + int(has_other) + has_up.astype(jnp.int32) + has_down.astype(jnp.int32)
    pl.semaphore_wait(barrier, count)
    load_k.wait()
    load_v.wait()

    @pl.when(own_up)
    def _():
        for p in range(PIECES):
            to_up(row, p, 0).start()

    if has_other:

        @pl.when(own_cross)
        def _():
            for p in range(PIECES):
                to_other(row, p, 0).start()

    @pl.when(own_mate)
    def _():
        to_mate(row, 0).start()

    first = (row * n_col + col) * shard
    qpos = first + lax.broadcasted_iota(jnp.int32, (1, shard), 1)

    def within(places):
        return (places >= begins) & (places < ends)

    lanes_of = lax.broadcasted_iota(jnp.int32, (1, HEAD_DIM), 1)
    begins = jnp.zeros((1, HEAD_DIM), jnp.int32)
    ends = jnp.full((1, HEAD_DIM), n_row * n_col * shard, jnp.int32)
    end = jnp.int32(0)
    docs = lens_ref.shape[0]
    for doc in range(docs):
        begins = jnp.where(lanes_of == doc, end, begins)
        end = end + lens_ref[doc]
        ends = jnp.where(lanes_of == doc, end, ends)
    offsets = lax.broadcasted_iota(jnp.int32, (shard, HEAD_DIM), 0)
    member = within(first + offsets) & (lanes_of < docs)
    member_ref[...] = jnp.where(member, 1.0, 0.0).astype(jnp.bfloat16)
    load_q.wait()

    def attend(blocks, fresh):
        count = shard * len(blocks)
        keys = jnp.concatenate([kv[at, which, :shard, :] for at, which in blocks], axis=0)
        vals = jnp.concatenate([kv[at, which, shard:, :] for at, which in blocks], axis=0)
        places = [at * tile + which * shard + offsets for at, which in blocks]
        apart = [jnp.where(within(place), 0.0, MASKED).astype(jnp.bfloat16) for place in places]
        kwide = jnp.concatenate([keys, jnp.concatenate(apart, axis=0)], axis=1)
        if fresh:
            kpos = first + lax.broadcasted_iota(jnp.int32, (count, shard), 0)
            bias = jnp.where(kpos <= qpos, jnp.float32(0.0), jnp.float32(MASKED))
        vflip = jnp.concatenate([vals.T, jnp.ones((SUM_ROWS, count), vals.dtype)], axis=0)

        def score(head):
            q = q_ref[:, head * HEAD_DIM : (head + 1) * HEAD_DIM]
            qwide = jnp.concatenate([q, member_ref[...]], axis=1)
            scores = lax.dot_general(
                kwide, qwide, (((1,), (1,)), ((), ())), preferred_element_type=jnp.float32
            )
            if fresh:
                scores = scores + bias
            s_ref[head % AHEAD_SLOTS, :count, :] = scores
            top = jnp.max(scores, axis=0, keepdims=True)
            if fresh:
                return top, top
            before = top_ref[head : head + 1, :]
            return before, jnp.maximum(before, top)

        tops = [score(head) for head in range(AHEAD_SLOTS - 1)]
        for head in range(heads):
            before, top = tops[head]
            if head + AHEAD_SLOTS - 1 < heads:
                tops.append(score(head + AHEAD_SLOTS - 1))
            weights = jnp.exp2((s_ref[head % AHEAD_SLOTS, :count, :] - top) * RATE)
            both = jnp.dot(vflip, weights.astype(jnp.bfloat16), preferred_element_type=jnp.float32)
            summed, total = both[:HEAD_DIM, :], both[HEAD_DIM : HEAD_DIM + 1, :]
            if not fresh:
                factor = jnp.exp2((before - top) * RATE)
                total = total + total_ref[head : head + 1, :] * factor
                summed = summed + acc_ref[head] * factor
            top_ref[head : head + 1, :] = top
            total_ref[head : head + 1, :] = total
            acc_ref[head] = summed

    attend([(row, col)], True)

    @pl.when(col > 0)
    def _():
        wait_whole(row, mate_sem.at[0])
        attend([(row, mate)], False)

    def relay(dist):
        near = straight(dist)

        @pl.when(needs(row, near))
        def _():
            up = has_up & needs(row + lanes, near)
            across = needs(other, near)
            for p in range(PIECES):
                wait_part(near, p, in_sem.at[2 * dist, p])

                @pl.when(up)
                def _():
                    to_up(near, p, dist).start()

                if has_other:

                    @pl.when(across)
                    def _():
                        to_other(near, p, dist).start()

            to_mate(near, 2 * dist).start()

        if has_other:
            far = crossed(dist - 1)

            @pl.when(needs(row, far))
            def _():
                for p in range(PIECES):
                    wait_part(far, p, in_sem.at[2 * dist - 1, p])
                to_mate(far, 2 * dist - 1).start()

    def drain(dist):
        near = straight(dist)

        @pl.when(needs(row, near))
        def _():
            @pl.when(has_up & needs(row + lanes, near))
            def _():
                wait_whole(near, up_send.at[dist])

            if has_other:

                @pl.when(needs(other, near))
                def _():
                    wait_whole(near, cross_send.at[dist])

            wait_whole(near, mate_send.at[2 * dist])

        if has_other:
            far = crossed(dist - 1)

            @pl.when(needs(row, far))
            def _():
                wait_whole(far, mate_send.at[2 * dist - 1])

    @pl.loop(1, furthest + 2)
    def _(dist):
        near, far = straight(dist), crossed(dist - 1)
        has_near = needs(row, near)
        has_far = needs(row, far) if has_other else jnp.bool_(False)
        both = has_near & has_far
        relay(dist)

        @pl.loop(0, 2)
        def _(half):
            waits = jnp.where(both, half == 1, half == 0)

            @pl.when(waits & has_near)
            def _():
                wait_whole(near, mate_sem.at[2 * dist])

            if has_other:

                @pl.when(waits & has_far)
                def _():
                    wait_whole(far, mate_sem.at[2 * dist - 1])

            @pl.when(both | ((half == 0) & (has_near | has_far)))
            def _():
                first_at = jnp.where(has_near, near, far)
                second_at = jnp.where(has_far, far, near)
                first_col = jnp.where(half == 0, col, mate)
                second_col = jnp.where(both & (half == 0), col, mate)
                attend([(first_at, first_col), (second_at, second_col)], False)

        drain(dist)

    for head in range(heads):
        inverse = 1.0 / total_ref[head : head + 1, :]
        result = (acc_ref[head] * inverse).T
        o_ref[:, head * HEAD_DIM : (head + 1) * HEAD_DIM] = result.astype(o_ref.dtype)

    @pl.when(own_up)
    def _():
        wait_whole(row, up_send.at[0])

    if has_other:

        @pl.when(own_cross)
        def _():
            wait_whole(row, cross_send.at[0])

    @pl.when(own_mate)
    def _():
        wait_whole(row, mate_send.at[0])


def shards(n_row, n_col, queries, keys, values, doc_lengths):
    shard, width = queries.shape
    lanes = 2 if n_row % 2 == 0 else 1
    span = shard * n_row * n_col
    longest = (3 * span) // 4
    reach = min(n_row - 1, -(-longest // (shard * n_col)))
    levels = n_row // lanes
    furthest = min(levels - 1, (reach + lanes - 1) // lanes)
    heads = width // HEAD_DIM
    vmem = pl.BlockSpec(memory_space=pltpu.VMEM)
    whole = pl.BlockSpec(memory_space=pltpu.HBM)
    units = 2 * furthest + 3
    return pl.pallas_call(
        functools.partial(kernel, n_row, n_col, lanes, reach),
        out_shape=jax.ShapeDtypeStruct(queries.shape, queries.dtype),
        in_specs=[pl.BlockSpec(memory_space=pltpu.SMEM), whole, whole, whole],
        out_specs=vmem,
        scratch_shapes=[
            pltpu.VMEM((n_row, n_col, 2 * shard, HEAD_DIM), keys.dtype),
            pltpu.VMEM((shard, width), queries.dtype),
            pltpu.VMEM((shard, HEAD_DIM), queries.dtype),
            pltpu.VMEM((heads, shard), jnp.float32),
            pltpu.VMEM((heads, shard), jnp.float32),
            pltpu.VMEM((heads, HEAD_DIM, shard), jnp.float32),
            pltpu.VMEM((AHEAD_SLOTS, n_col * shard, shard), jnp.float32),
            pltpu.SemaphoreType.DMA((3,)),
            pltpu.SemaphoreType.DMA((units, PIECES)),
            pltpu.SemaphoreType.DMA((units,)),
            pltpu.SemaphoreType.DMA((furthest + 2,)),
            pltpu.SemaphoreType.DMA((furthest + 2,)),
            pltpu.SemaphoreType.DMA((units,)),
        ],
        compiler_params=pltpu.CompilerParams(
            collective_id=0, has_side_effects=True, vmem_limit_bytes=24 << 20
        ),
        name="attend",
    )(*(pltpu.with_memory_space_constraint(x, pltpu.HBM) for x in (doc_lengths, queries, keys, values)))


def solution(mesh):
    placed = P(("groups", "row", "col"), None)
    return jax.shard_map(
        functools.partial(shards, mesh.shape["row"], mesh.shape["col"]),
        mesh=mesh,
        in_specs=(placed, placed, placed, P("groups")),
        out_specs=placed,
        check_vma=False,
    )
```

```python
import functools

import jax
import jax.numpy as jnp
from jax import lax
from jax.experimental import pallas as pl
from jax.experimental.pallas import tpu as pltpu
from jax.sharding import PartitionSpec as P

HEAD_DIM = 128
RATE = HEAD_DIM ** (-0.5) * 1.4426950408889634
MASKED = -1e30
AHEAD_SLOTS = 8
SUM_ROWS = 16
PIECES = 2


def kernel(
    n_row,
    n_col,
    lanes,
    reach,
    lens_hbm,
    q_hbm,
    k_hbm,
    v_hbm,
    o_ref,
    lens_ref,
    kv,
    q_ref,
    member_ref,
    top_ref,
    total_ref,
    acc_ref,
    s_ref,
    load_sem,
    in_sem,
    mate_sem,
    up_send,
    cross_send,
    mate_send,
):
    shard = q_hbm.shape[0]
    heads = q_hbm.shape[1] // HEAD_DIM
    levels = n_row // lanes
    tile = n_col * shard
    piece = 2 * shard // PIECES
    furthest = min(levels - 1, (reach + lanes - 1) // lanes)
    has_other = lanes > 1
    row = lax.axis_index("row")
    col = lax.axis_index("col")
    level = row // lanes
    lane = row % lanes
    mate = 1 - col
    other = level * lanes + (lanes - 1 - lane)
    has_up = level + 1 < levels
    has_down = level > 0

    def needs(reader, source):
        return (source >= 0) & (reader > source) & (reader - source <= reach)

    def straight(dist):
        return row - dist * lanes

    def crossed(dist):
        return other - dist * lanes

    barrier = pltpu.get_barrier_semaphore()
    pl.semaphore_signal(barrier, inc=1, device_id={"col": mate})
    if has_other:
        pl.semaphore_signal(barrier, inc=1, device_id={"row": other})

    @pl.when(has_up)
    def _():
        pl.semaphore_signal(barrier, inc=1, device_id={"row": row + lanes})

    @pl.when(has_down)
    def _():
        pl.semaphore_signal(barrier, inc=1, device_id={"row": row - lanes})

    load_k = pltpu.make_async_copy(k_hbm, kv.at[row, col, :shard, :], load_sem.at[0])
    load_v = pltpu.make_async_copy(v_hbm, kv.at[row, col, shard:, :], load_sem.at[1])
    load_q = pltpu.make_async_copy(q_hbm, q_ref, load_sem.at[2])
    load_lens = pltpu.make_async_copy(lens_hbm, lens_ref, load_sem.at[3])
    for load in (load_k, load_v, load_q, load_lens):
        load.start()

    def copy(source, rows, send_sem, recv_sem, device):
        here = kv.at[source, col, rows, :]
        return pltpu.make_async_remote_copy(
            src_ref=here,
            dst_ref=here,
            send_sem=send_sem,
            recv_sem=recv_sem,
            device_id=device,
            device_id_type=pl.DeviceIdType.MESH,
        )

    def part(p):
        return pl.ds(p * piece, piece)

    def to_up(source, p, dist):
        recv = in_sem.at[2 * dist + 2, p]
        return copy(source, part(p), up_send.at[dist], recv, {"row": row + lanes})

    def to_other(source, p, dist):
        recv = in_sem.at[2 * dist + 1, p]
        return copy(source, part(p), cross_send.at[dist], recv, {"row": other})

    def to_mate(source, p, unit):
        return copy(source, part(p), mate_send.at[unit], mate_sem.at[unit], {"col": mate})

    def wait_whole(source, sem):
        here = kv.at[source, col, :, :]
        pltpu.make_async_copy(here, here, sem).wait()

    def wait_part(source, p, sem):
        here = kv.at[source, col, part(p), :]
        pltpu.make_async_copy(here, here, sem).wait()

    own_up = has_up
    own_cross = needs(other, row)
    own_mate = col < mate

    count = 1 + int(has_other) + has_up.astype(jnp.int32) + has_down.astype(jnp.int32)
    pl.semaphore_wait(barrier, count)
    load_k.wait()
    load_v.wait()

    @pl.when(own_up)
    def _():
        for p in range(PIECES):
            to_up(row, p, 0).start()

    if has_other:

        @pl.when(own_cross)
        def _():
            for p in range(PIECES):
                to_other(row, p, 0).start()

    @pl.when(own_mate)
    def _():
        for p in range(PIECES):
            to_mate(row, p, 0).start()

    first = (row * n_col + col) * shard
    qpos = first + lax.broadcasted_iota(jnp.int32, (1, shard), 1)

    def within(places):
        return (places >= begins) & (places < ends)

    lanes_of = lax.broadcasted_iota(jnp.int32, (1, HEAD_DIM), 1)
    begins = jnp.zeros((1, HEAD_DIM), jnp.int32)
    ends = jnp.full((1, HEAD_DIM), n_row * n_col * shard, jnp.int32)
    end = jnp.int32(0)
    load_lens.wait()
    docs = lens_ref.shape[0]
    for doc in range(docs):
        begins = jnp.where(lanes_of == doc, end, begins)
        end = end + lens_ref[doc]
        ends = jnp.where(lanes_of == doc, end, ends)
    offsets = lax.broadcasted_iota(jnp.int32, (shard, HEAD_DIM), 0)
    member = within(first + offsets) & (lanes_of < docs)
    member_ref[...] = jnp.where(member, 1.0, 0.0).astype(jnp.bfloat16)
    load_q.wait()

    def attend(blocks, fresh):
        count = shard * len(blocks)
        keys = jnp.concatenate([kv[at, which, :shard, :] for at, which in blocks], axis=0)
        vals = jnp.concatenate([kv[at, which, shard:, :] for at, which in blocks], axis=0)
        places = [at * tile + which * shard + offsets for at, which in blocks]
        apart = [jnp.where(within(place), 0.0, MASKED).astype(jnp.bfloat16) for place in places]
        kwide = jnp.concatenate([keys, jnp.concatenate(apart, axis=0)], axis=1)
        if fresh:
            kpos = first + lax.broadcasted_iota(jnp.int32, (count, shard), 0)
            bias = jnp.where(kpos <= qpos, jnp.float32(0.0), jnp.float32(MASKED))
        vflip = jnp.concatenate([vals.T, jnp.ones((SUM_ROWS, count), vals.dtype)], axis=0)

        def score(head):
            q = q_ref[:, head * HEAD_DIM : (head + 1) * HEAD_DIM]
            qwide = jnp.concatenate([q, member_ref[...]], axis=1)
            scores = lax.dot_general(
                kwide, qwide, (((1,), (1,)), ((), ())), preferred_element_type=jnp.float32
            )
            if fresh:
                scores = scores + bias
            s_ref[head % AHEAD_SLOTS, :count, :] = scores
            top = jnp.max(scores, axis=0, keepdims=True)
            if fresh:
                return top, top
            before = top_ref[head : head + 1, :]
            return before, jnp.maximum(before, top)

        tops = [score(head) for head in range(AHEAD_SLOTS - 1)]
        for head in range(heads):
            before, top = tops[head]
            if head + AHEAD_SLOTS - 1 < heads:
                tops.append(score(head + AHEAD_SLOTS - 1))
            weights = jnp.exp2((s_ref[head % AHEAD_SLOTS, :count, :] - top) * RATE)
            both = jnp.dot(vflip, weights.astype(jnp.bfloat16), preferred_element_type=jnp.float32)
            summed, total = both[:HEAD_DIM, :], both[HEAD_DIM : HEAD_DIM + 1, :]
            if not fresh:
                factor = jnp.exp2((before - top) * RATE)
                total = total + total_ref[head : head + 1, :] * factor
                summed = summed + acc_ref[head] * factor
            top_ref[head : head + 1, :] = top
            total_ref[head : head + 1, :] = total
            acc_ref[head] = summed

    attend([(row, col)], True)

    @pl.when(col > 0)
    def _():
        wait_whole(row, mate_sem.at[0])
        attend([(row, mate)], False)

    def relay(dist):
        near = straight(dist)

        @pl.when(needs(row, near))
        def _():
            up = has_up & needs(row + lanes, near)
            across = needs(other, near)
            for p in range(PIECES):
                wait_part(near, p, in_sem.at[2 * dist, p])

                @pl.when(up)
                def _():
                    to_up(near, p, dist).start()

                if has_other:

                    @pl.when(across)
                    def _():
                        to_other(near, p, dist).start()

                to_mate(near, p, 2 * dist).start()

        if has_other:
            far = crossed(dist - 1)

            @pl.when(needs(row, far))
            def _():
                for p in range(PIECES):
                    wait_part(far, p, in_sem.at[2 * dist - 1, p])
                    to_mate(far, p, 2 * dist - 1).start()

    def drain_own():
        @pl.when(own_up)
        def _():
            wait_whole(row, up_send.at[0])

        if has_other:

            @pl.when(own_cross)
            def _():
                wait_whole(row, cross_send.at[0])

        @pl.when(own_mate)
        def _():
            wait_whole(row, mate_send.at[0])

    def drain(dist):
        near = straight(dist)

        @pl.when(needs(row, near))
        def _():
            @pl.when(has_up & needs(row + lanes, near))
            def _():
                wait_whole(near, up_send.at[dist])

            if has_other:

                @pl.when(needs(other, near))
                def _():
                    wait_whole(near, cross_send.at[dist])

            wait_whole(near, mate_send.at[2 * dist])

        if has_other:
            far = crossed(dist - 1)

            @pl.when(needs(row, far))
            def _():
                wait_whole(far, mate_send.at[2 * dist - 1])

    @pl.loop(1, furthest + 2)
    def _(dist):
        near, far = straight(dist), crossed(dist - 1)
        has_near = needs(row, near)
        has_far = needs(row, far) if has_other else jnp.bool_(False)
        both = has_near & has_far
        relay(dist)

        @pl.when(dist == 2)
        def _():
            drain_own()

        @pl.when(dist > 1)
        def _():
            drain(dist - 1)

        single = jnp.where(has_near, near, far)
        single_unit = jnp.where(has_near, 2 * dist, 2 * dist - 1)
        alone = has_near != has_far

        @pl.loop(0, 2)
        def _(half):
            which = jnp.where(half == 0, col, mate)

            @pl.when(both)
            def _():
                @pl.when(half == 1)
                def _():
                    wait_whole(near, mate_sem.at[2 * dist])
                    if has_other:
                        wait_whole(far, mate_sem.at[2 * dist - 1])

                attend([(near, which), (far, which)], False)

            @pl.when(alone)
            def _():
                @pl.when(half == 1)
                def _():
                    wait_whole(single, mate_sem.at[single_unit])

                attend([(single, which)], False)

    for head in range(heads):
        inverse = 1.0 / total_ref[head : head + 1, :]
        result = (acc_ref[head] * inverse).T
        o_ref[:, head * HEAD_DIM : (head + 1) * HEAD_DIM] = result.astype(o_ref.dtype)

    drain(furthest + 1)


def shards(n_row, n_col, queries, keys, values, doc_lengths):
    shard, width = queries.shape
    lanes = 2 if n_row % 2 == 0 else 1
    span = shard * n_row * n_col
    longest = (3 * span) // 4
    reach = min(n_row - 1, -(-longest // (shard * n_col)))
    levels = n_row // lanes
    furthest = min(levels - 1, (reach + lanes - 1) // lanes)
    heads = width // HEAD_DIM
    vmem = pl.BlockSpec(memory_space=pltpu.VMEM)
    whole = pl.BlockSpec(memory_space=pltpu.HBM)
    units = 2 * furthest + 3
    return pl.pallas_call(
        functools.partial(kernel, n_row, n_col, lanes, reach),
        out_shape=jax.ShapeDtypeStruct(queries.shape, queries.dtype),
        in_specs=[whole, whole, whole, whole],
        out_specs=vmem,
        scratch_shapes=[
            pltpu.SMEM(doc_lengths.shape, doc_lengths.dtype),
            pltpu.VMEM((n_row, n_col, 2 * shard, HEAD_DIM), keys.dtype),
            pltpu.VMEM((shard, width), queries.dtype),
            pltpu.VMEM((shard, HEAD_DIM), queries.dtype),
            pltpu.VMEM((heads, shard), jnp.float32),
            pltpu.VMEM((heads, shard), jnp.float32),
            pltpu.VMEM((heads, HEAD_DIM, shard), jnp.float32),
            pltpu.VMEM((AHEAD_SLOTS, n_col * shard, shard), jnp.float32),
            pltpu.SemaphoreType.DMA((4,)),
            pltpu.SemaphoreType.DMA((units, PIECES)),
            pltpu.SemaphoreType.DMA((units,)),
            pltpu.SemaphoreType.DMA((furthest + 2,)),
            pltpu.SemaphoreType.DMA((furthest + 2,)),
            pltpu.SemaphoreType.DMA((units,)),
        ],
        compiler_params=pltpu.CompilerParams(
            collective_id=0, has_side_effects=True, vmem_limit_bytes=24 << 20
        ),
        name="attend",
    )(*(pltpu.with_memory_space_constraint(x, pltpu.HBM) for x in (doc_lengths, queries, keys, values)))


def solution(mesh):
    placed = P(("groups", "row", "col"), None)
    return jax.shard_map(
        functools.partial(shards, mesh.shape["row"], mesh.shape["col"]),
        mesh=mesh,
        in_specs=(placed, placed, placed, P("groups")),
        out_specs=placed,
        check_vma=False,
    )
```

```python
import functools

import jax
import jax.numpy as jnp
from jax import lax
from jax.experimental import pallas as pl
from jax.experimental.pallas import tpu as pltpu
from jax.sharding import PartitionSpec as P

HEAD_DIM = 128
RATE = HEAD_DIM ** (-0.5) * 1.4426950408889634
MASKED = -1e30
AHEAD_SLOTS = 8
SUM_ROWS = 16
CUTS = (0, 1, 2)
PIECES = len(CUTS) - 1


def kernel(
    n_row,
    n_col,
    lanes,
    reach,
    lens_hbm,
    q_hbm,
    k_hbm,
    v_hbm,
    o_ref,
    lens_ref,
    kv,
    q_ref,
    member_ref,
    top_ref,
    total_ref,
    acc_ref,
    s_ref,
    load_sem,
    in_sem,
    mate_sem,
    up_send,
    cross_send,
    mate_send,
    far_send,
):
    shard = q_hbm.shape[0]
    heads = q_hbm.shape[1] // HEAD_DIM
    levels = n_row // lanes
    tile = n_col * shard
    cuts = [2 * shard * cut // CUTS[-1] for cut in CUTS]
    furthest = min(levels - 1, (reach + lanes - 1) // lanes)
    has_other = lanes > 1
    row = lax.axis_index("row")
    col = lax.axis_index("col")
    level = row // lanes
    lane = row % lanes
    mate = 1 - col
    other = level * lanes + (lanes - 1 - lane)
    has_up = level + 1 < levels
    has_down = level > 0

    def needs(reader, source):
        return (source >= 0) & (reader > source) & (reader - source <= reach)

    def straight(dist):
        return row - dist * lanes

    def crossed(dist):
        return other - dist * lanes

    barrier = pltpu.get_barrier_semaphore()
    pl.semaphore_signal(barrier, inc=1, device_id={"col": mate})
    if has_other:
        pl.semaphore_signal(barrier, inc=1, device_id={"row": other})

    @pl.when(has_up)
    def _():
        pl.semaphore_signal(barrier, inc=1, device_id={"row": row + lanes})

    @pl.when(has_down)
    def _():
        pl.semaphore_signal(barrier, inc=1, device_id={"row": row - lanes})

    load_k = pltpu.make_async_copy(k_hbm, kv.at[row, col, :shard, :], load_sem.at[0])
    load_v = pltpu.make_async_copy(v_hbm, kv.at[row, col, shard:, :], load_sem.at[0])
    load_q = pltpu.make_async_copy(q_hbm, q_ref, load_sem.at[1])
    load_lens = pltpu.make_async_copy(lens_hbm, lens_ref, load_sem.at[2])
    for load in (load_k, load_v, load_q, load_lens):
        load.start()

    def copy(source, rows, send_sem, recv_sem, device):
        here = kv.at[source, col, rows, :]
        return pltpu.make_async_remote_copy(
            src_ref=here,
            dst_ref=here,
            send_sem=send_sem,
            recv_sem=recv_sem,
            device_id=device,
            device_id_type=pl.DeviceIdType.MESH,
        )

    def part(p):
        return pl.ds(cuts[p], cuts[p + 1] - cuts[p])

    def to_up(source, p, dist):
        recv = in_sem.at[2 * dist + 1, p]
        return copy(source, part(p), up_send.at[dist % 2], recv, {"row": row + lanes})

    def to_other(source, p, dist):
        recv = in_sem.at[2 * dist, p]
        return copy(source, part(p), cross_send.at[dist % 2], recv, {"row": other})

    split_level = levels - 3
    late_from = PIECES // 2
    splits = has_other and split_level >= 0

    def split(source):
        return source == split_level * lanes + lanes - 1

    def far_up(source):
        return split(source) & has_up & needs(row + lanes, source)

    def to_far_up(source, p, dist):
        recv = in_sem.at[2 * dist + 2, p]
        return copy(source, part(p), far_send.at[0], recv, {"row": row + lanes})

    def wait_rows(source, start, stop, sem):
        here = kv.at[source, col, start:stop, :]
        pltpu.make_async_copy(here, here, sem).wait()

    def to_mate(source, p, unit):
        return copy(source, part(p), mate_send.at[unit % 4], mate_sem.at[unit], {"col": mate})

    def wait_whole(source, sem):
        here = kv.at[source, col, :, :]
        pltpu.make_async_copy(here, here, sem).wait()

    def wait_part(source, p, sem):
        here = kv.at[source, col, part(p), :]
        pltpu.make_async_copy(here, here, sem).wait()

    own_up = has_up
    own_cross = needs(other, row)
    own_mate = col < mate

    count = 1 + int(has_other) + has_up.astype(jnp.int32) + has_down.astype(jnp.int32)
    pl.semaphore_wait(barrier, count)
    wait_whole(row, load_sem.at[0])

    @pl.when(own_up)
    def _():
        for p in range(PIECES):
            to_up(row, p, 0).start()

    if has_other:

        @pl.when(own_cross)
        def _():
            for p in range(PIECES):
                to_other(row, p, 0).start()

    if splits:

        @pl.when(split(row) & has_up)
        def _():
            for p in range(late_from, PIECES):
                to_other(row, p, 0).start()

    @pl.when(own_mate)
    def _():
        for p in range(PIECES):
            to_mate(row, p, 0).start()

    first = (row * n_col + col) * shard
    qpos = first + lax.broadcasted_iota(jnp.int32, (1, shard), 1)

    def within(places):
        return (places >= begins) & (places < ends)

    lanes_of = lax.broadcasted_iota(jnp.int32, (1, HEAD_DIM), 1)
    begins = jnp.zeros((1, HEAD_DIM), jnp.int32)
    ends = jnp.full((1, HEAD_DIM), n_row * n_col * shard, jnp.int32)
    end = jnp.int32(0)
    load_lens.wait()
    docs = lens_ref.shape[0]
    for doc in range(docs):
        begins = jnp.where(lanes_of == doc, end, begins)
        end = end + lens_ref[doc]
        ends = jnp.where(lanes_of == doc, end, ends)
    offsets = lax.broadcasted_iota(jnp.int32, (shard, HEAD_DIM), 0)
    member = within(first + offsets) & (lanes_of < docs)
    member_ref[...] = jnp.where(member, 1.0, 0.0).astype(jnp.bfloat16)
    load_q.wait()

    def attend(blocks, fresh):
        count = shard * len(blocks)
        keys = jnp.concatenate([kv[at, which, :shard, :] for at, which in blocks], axis=0)
        vals = jnp.concatenate([kv[at, which, shard:, :] for at, which in blocks], axis=0)
        places = [at * tile + which * shard + offsets for at, which in blocks]
        apart = [jnp.where(within(place), 0.0, MASKED).astype(jnp.bfloat16) for place in places]
        kwide = jnp.concatenate([keys, jnp.concatenate(apart, axis=0)], axis=1)
        if fresh:
            kpos = first + lax.broadcasted_iota(jnp.int32, (count, shard), 0)
            bias = jnp.where(kpos <= qpos, jnp.float32(0.0), jnp.float32(MASKED))
        vflip = jnp.concatenate([vals.T, jnp.ones((SUM_ROWS, count), vals.dtype)], axis=0)

        def score(head):
            q = q_ref[:, head * HEAD_DIM : (head + 1) * HEAD_DIM]
            qwide = jnp.concatenate([q, member_ref[...]], axis=1)
            scores = lax.dot_general(
                kwide, qwide, (((1,), (1,)), ((), ())), preferred_element_type=jnp.float32
            )
            if fresh:
                scores = scores + bias
            s_ref[head % AHEAD_SLOTS, :count, :] = scores
            top = jnp.max(scores, axis=0, keepdims=True)
            if fresh:
                return top, top
            before = top_ref[head : head + 1, :]
            return before, jnp.maximum(before, top)

        tops = [score(head) for head in range(AHEAD_SLOTS - 1)]
        for head in range(heads):
            before, top = tops[head]
            if head + AHEAD_SLOTS - 1 < heads:
                tops.append(score(head + AHEAD_SLOTS - 1))
            weights = jnp.exp2((s_ref[head % AHEAD_SLOTS, :count, :] - top) * RATE)
            both = jnp.dot(vflip, weights.astype(jnp.bfloat16), preferred_element_type=jnp.float32)
            summed, total = both[:HEAD_DIM, :], both[HEAD_DIM : HEAD_DIM + 1, :]
            if not fresh:
                factor = jnp.exp2((before - top) * RATE)
                total = total + total_ref[head : head + 1, :] * factor
                summed = summed + acc_ref[head] * factor
            top_ref[head : head + 1, :] = top
            total_ref[head : head + 1, :] = total
            acc_ref[head] = summed

    attend([(row, col)], True)

    @pl.when(col > 0)
    def _():
        wait_whole(row, mate_sem.at[0])
        attend([(row, mate)], False)

    def relay_near(dist):
        near = straight(dist)

        @pl.when(needs(row, near))
        def _():
            up = has_up & needs(row + lanes, near)
            across = needs(other, near)
            across_late = across & jnp.logical_not(split(near)) if splits else across
            for p in range(PIECES):
                wait_part(near, p, in_sem.at[2 * dist - 1, p])

                @pl.when(up)
                def _():
                    to_up(near, p, dist).start()

                if has_other:

                    @pl.when(across_late if p >= late_from else across)
                    def _():
                        to_other(near, p, dist).start()

                to_mate(near, p, 2 * dist).start()

    def relay_far(dist):
        far = crossed(dist)

        @pl.when(needs(row, far))
        def _():
            for p in range(PIECES):
                wait_part(far, p, in_sem.at[2 * dist, p])
                if splits and p >= late_from:

                    @pl.when(far_up(far))
                    def _():
                        to_far_up(far, p, dist).start()

                to_mate(far, p, 2 * dist + 1).start()

        if splits:

            @pl.when((far > row) & far_up(far))
            def _():
                for p in range(late_from, PIECES):
                    wait_part(far, p, in_sem.at[2 * dist, p])
                    to_far_up(far, p, dist).start()

    def early(dist):
        return (lane == lanes - 1) & (level == dist + 1) & (dist >= 1)

    def drain_own():
        @pl.when(own_up)
        def _():
            wait_whole(row, up_send.at[0])

        if has_other:

            @pl.when(own_cross)
            def _():
                wait_whole(row, cross_send.at[0])

        if splits:

            @pl.when(split(row) & has_up)
            def _():
                wait_rows(row, cuts[late_from], cuts[-1], cross_send.at[0])

        @pl.when(own_mate)
        def _():
            wait_whole(row, mate_send.at[0])

    def drain(dist):
        near = straight(dist)

        @pl.when(needs(row, near))
        def _():
            @pl.when(has_up & needs(row + lanes, near))
            def _():
                wait_whole(near, up_send.at[dist % 2])

            if has_other:

                if splits:

                    @pl.when(needs(other, near) & split(near))
                    def _():
                        wait_rows(near, 0, cuts[late_from], cross_send.at[dist % 2])

                @pl.when(needs(other, near) & jnp.logical_not(split(near)) if splits else needs(other, near))
                def _():
                    wait_whole(near, cross_send.at[dist % 2])

            wait_whole(near, mate_send.at[2 * dist % 4])

        if has_other:
            far = crossed(dist - 1)

            @pl.when(needs(row, far))
            def _():
                wait_whole(far, mate_send.at[(2 * dist - 1) % 4])

            if splits:

                @pl.when(far_up(far))
                def _():
                    wait_rows(far, cuts[late_from], cuts[-1], far_send.at[0])

    @pl.loop(1, furthest + 2)
    def _(dist):
        near, far = straight(dist), crossed(dist - 1)
        has_near = needs(row, near)
        has_far = needs(row, far) if has_other else jnp.bool_(False)
        both = has_near & has_far
        @pl.when(jnp.logical_not(early(dist - 1)))
        def _():
            relay_near(dist)

        if has_other:
            relay_far(dist - 1)

        @pl.when(dist == 1)
        def _():
            drain_own()

        @pl.when(dist > 1)
        def _():
            drain(dist - 1)

        single = jnp.where(has_near, near, far)
        single_unit = jnp.where(has_near, 2 * dist, 2 * dist - 1)
        alone = has_near != has_far

        @pl.loop(0, 2)
        def _(half):
            which = jnp.where(half == 0, col, mate)

            @pl.when(both)
            def _():
                @pl.when(half == 1)
                def _():
                    wait_whole(near, mate_sem.at[2 * dist])
                    if has_other:
                        wait_whole(far, mate_sem.at[2 * dist - 1])

                attend([(near, which), (far, which)], False)

            @pl.when((half == 0) & early(dist))
            def _():
                relay_near(dist + 1)

            @pl.when(alone)
            def _():
                @pl.when(half == 1)
                def _():
                    wait_whole(single, mate_sem.at[single_unit])

                attend([(single, which)], False)

    for head in range(heads):
        inverse = 1.0 / total_ref[head : head + 1, :]
        result = (acc_ref[head] * inverse).T
        o_ref[:, head * HEAD_DIM : (head + 1) * HEAD_DIM] = result.astype(o_ref.dtype)

    drain(furthest + 1)


def shards(n_row, n_col, queries, keys, values, doc_lengths):
    shard, width = queries.shape
    lanes = 2 if n_row % 2 == 0 else 1
    span = shard * n_row * n_col
    longest = (3 * span) // 4
    reach = min(n_row - 1, -(-longest // (shard * n_col)))
    levels = n_row // lanes
    furthest = min(levels - 1, (reach + lanes - 1) // lanes)
    heads = width // HEAD_DIM
    vmem = pl.BlockSpec(memory_space=pltpu.VMEM)
    whole = pl.BlockSpec(memory_space=pltpu.HBM)
    units = 2 * furthest + 2
    return pl.pallas_call(
        functools.partial(kernel, n_row, n_col, lanes, reach),
        out_shape=jax.ShapeDtypeStruct(queries.shape, queries.dtype),
        in_specs=[whole, whole, whole, whole],
        out_specs=vmem,
        scratch_shapes=[
            pltpu.SMEM(doc_lengths.shape, doc_lengths.dtype),
            pltpu.VMEM((n_row, n_col, 2 * shard, HEAD_DIM), keys.dtype),
            pltpu.VMEM((shard, width), queries.dtype),
            pltpu.VMEM((shard, HEAD_DIM), queries.dtype),
            pltpu.VMEM((heads, shard), jnp.float32),
            pltpu.VMEM((heads, shard), jnp.float32),
            pltpu.VMEM((heads, HEAD_DIM, shard), jnp.float32),
            pltpu.VMEM((AHEAD_SLOTS, n_col * shard, shard), jnp.float32),
            pltpu.SemaphoreType.DMA((3,)),
            pltpu.SemaphoreType.DMA((units - 1, PIECES)),
            pltpu.SemaphoreType.DMA((units,)),
            pltpu.SemaphoreType.DMA((2,)),
            pltpu.SemaphoreType.DMA((2,)),
            pltpu.SemaphoreType.DMA((4,)),
            pltpu.SemaphoreType.DMA((1,)),
        ],
        compiler_params=pltpu.CompilerParams(
            collective_id=0, has_side_effects=True, vmem_limit_bytes=24 << 20
        ),
        name="attend",
    )(*(pltpu.with_memory_space_constraint(x, pltpu.HBM) for x in (doc_lengths, queries, keys, values)))


def solution(mesh):
    placed = P(("groups", "row", "col"), None)
    return jax.shard_map(
        functools.partial(shards, mesh.shape["row"], mesh.shape["col"]),
        mesh=mesh,
        in_specs=(placed, placed, placed, P("groups")),
        out_specs=placed,
        check_vma=False,
    )
```

```python
import functools

import jax
import jax.numpy as jnp
from jax import lax
from jax.experimental import pallas as pl
from jax.experimental.pallas import tpu as pltpu
from jax.sharding import PartitionSpec as P

HEAD_DIM = 128
RATE = HEAD_DIM ** (-0.5) * 1.4426950408889634
MASKED = -1e30
AHEAD_SLOTS = 7
SUM_ROWS = 16
CUTS = (0, 1, 2)
PIECES = len(CUTS) - 1


def kernel(
    n_row,
    n_col,
    lanes,
    reach,
    lens_hbm,
    q_hbm,
    k_hbm,
    v_hbm,
    o_ref,
    lens_ref,
    kv,
    q_ref,
    member_ref,
    top_ref,
    total_ref,
    acc_ref,
    s_ref,
    load_sem,
    in_sem,
    mate_sem,
    up_send,
    cross_send,
    mate_send,
    far_send,
):
    shard = q_hbm.shape[0]
    heads = q_hbm.shape[1] // HEAD_DIM
    levels = n_row // lanes
    tile = n_col * shard
    cuts = [2 * shard * cut // CUTS[-1] for cut in CUTS]
    furthest = min(levels - 1, (reach + lanes - 1) // lanes)
    has_other = lanes > 1
    row = lax.axis_index("row")
    col = lax.axis_index("col")
    level = row // lanes
    lane = row % lanes
    mate = 1 - col
    other = level * lanes + (lanes - 1 - lane)
    has_up = level + 1 < levels
    has_down = level > 0

    def needs(reader, source):
        return (source >= 0) & (reader > source) & (reader - source <= reach)

    def straight(dist):
        return row - dist * lanes

    def crossed(dist):
        return other - dist * lanes

    barrier = pltpu.get_barrier_semaphore()
    pl.semaphore_signal(barrier, inc=1, device_id={"col": mate})
    if has_other:
        pl.semaphore_signal(barrier, inc=1, device_id={"row": other})

    @pl.when(has_up)
    def _():
        pl.semaphore_signal(barrier, inc=1, device_id={"row": row + lanes})

    @pl.when(has_down)
    def _():
        pl.semaphore_signal(barrier, inc=1, device_id={"row": row - lanes})

    load_k = pltpu.make_async_copy(k_hbm, kv.at[row, col, :shard, :], load_sem.at[0])
    load_v = pltpu.make_async_copy(v_hbm, kv.at[row, col, shard:, :], load_sem.at[0])
    load_q = pltpu.make_async_copy(q_hbm, q_ref, load_sem.at[1])
    load_lens = pltpu.make_async_copy(lens_hbm, lens_ref, load_sem.at[2])
    for load in (load_k, load_v, load_q, load_lens):
        load.start()

    def copy(source, rows, send_sem, recv_sem, device):
        here = kv.at[source, col, rows, :]
        return pltpu.make_async_remote_copy(
            src_ref=here,
            dst_ref=here,
            send_sem=send_sem,
            recv_sem=recv_sem,
            device_id=device,
            device_id_type=pl.DeviceIdType.MESH,
        )

    def part(p):
        return pl.ds(cuts[p], cuts[p + 1] - cuts[p])

    def to_up(source, p, dist):
        recv = in_sem.at[2 * dist + 1, p]
        return copy(source, part(p), up_send.at[dist % 2], recv, {"row": row + lanes})

    def to_other(source, p, dist):
        recv = in_sem.at[2 * dist, p]
        return copy(source, part(p), cross_send.at[dist % 2], recv, {"row": other})

    split_level = levels - 3
    late_from = PIECES // 2
    splits = has_other and split_level >= 0

    def split(source):
        return source == split_level * lanes + lanes - 1

    def far_up(source):
        return split(source) & has_up & needs(row + lanes, source)

    def to_far_up(source, p, dist):
        recv = in_sem.at[2 * dist + 2, p]
        return copy(source, part(p), far_send.at[0], recv, {"row": row + lanes})

    def wait_rows(source, start, stop, sem):
        here = kv.at[source, col, start:stop, :]
        pltpu.make_async_copy(here, here, sem).wait()

    def to_mate(source, p, unit):
        return copy(source, part(p), mate_send.at[unit % 4], mate_sem.at[unit], {"col": mate})

    def wait_whole(source, sem):
        here = kv.at[source, col, :, :]
        pltpu.make_async_copy(here, here, sem).wait()

    def wait_part(source, p, sem):
        here = kv.at[source, col, part(p), :]
        pltpu.make_async_copy(here, here, sem).wait()

    own_up = has_up
    own_cross = needs(other, row)
    own_mate = col < mate

    count = 1 + int(has_other) + has_up.astype(jnp.int32) + has_down.astype(jnp.int32)
    pl.semaphore_wait(barrier, count)
    wait_whole(row, load_sem.at[0])

    @pl.when(own_up)
    def _():
        for p in range(PIECES):
            to_up(row, p, 0).start()

    if has_other:

        @pl.when(own_cross)
        def _():
            for p in range(PIECES):
                to_other(row, p, 0).start()

    if splits:

        @pl.when(split(row) & has_up)
        def _():
            for p in range(late_from, PIECES):
                to_other(row, p, 0).start()

    @pl.when(own_mate)
    def _():
        for p in range(PIECES):
            to_mate(row, p, 0).start()

    first = (row * n_col + col) * shard
    qpos = first + lax.broadcasted_iota(jnp.int32, (1, shard), 1)

    def within(places):
        return (places >= begins) & (places < ends)

    lanes_of = lax.broadcasted_iota(jnp.int32, (1, HEAD_DIM), 1)
    begins = jnp.zeros((1, HEAD_DIM), jnp.int32)
    ends = jnp.full((1, HEAD_DIM), n_row * n_col * shard, jnp.int32)
    end = jnp.int32(0)
    load_lens.wait()
    docs = lens_ref.shape[0]
    for doc in range(docs):
        begins = jnp.where(lanes_of == doc, end, begins)
        end = end + lens_ref[doc]
        ends = jnp.where(lanes_of == doc, end, ends)
    offsets = lax.broadcasted_iota(jnp.int32, (shard, HEAD_DIM), 0)
    member = within(first + offsets) & (lanes_of < docs)
    member_ref[...] = jnp.where(member, 1.0, 0.0).astype(jnp.bfloat16)
    load_q.wait()

    def attend(blocks, fresh):
        count = shard * len(blocks)
        keys = jnp.concatenate([kv[at, which, :shard, :] for at, which in blocks], axis=0)
        vals = jnp.concatenate([kv[at, which, shard:, :] for at, which in blocks], axis=0)
        places = [at * tile + which * shard + offsets for at, which in blocks]
        apart = [jnp.where(within(place), 0.0, MASKED).astype(jnp.bfloat16) for place in places]
        kwide = jnp.concatenate([keys, jnp.concatenate(apart, axis=0)], axis=1)
        if fresh:
            kpos = first + lax.broadcasted_iota(jnp.int32, (count, shard), 0)
            bias = jnp.where(kpos <= qpos, jnp.float32(0.0), jnp.float32(MASKED))
        vflip = jnp.concatenate([vals.T, jnp.ones((SUM_ROWS, count), vals.dtype)], axis=0)

        def score(head):
            q = q_ref[:, head * HEAD_DIM : (head + 1) * HEAD_DIM]
            qwide = jnp.concatenate([q, member_ref[...]], axis=1)
            scores = lax.dot_general(
                kwide, qwide, (((1,), (1,)), ((), ())), preferred_element_type=jnp.float32
            )
            if fresh:
                scores = scores + bias
            s_ref[head % AHEAD_SLOTS, :count, :] = scores
            top = jnp.max(scores, axis=0, keepdims=True)
            if fresh:
                return top, top
            before = top_ref[head : head + 1, :]
            return before, jnp.maximum(before, top)

        tops = [score(head) for head in range(AHEAD_SLOTS - 1)]
        for head in range(heads):
            before, top = tops[head]
            if head + AHEAD_SLOTS - 1 < heads:
                tops.append(score(head + AHEAD_SLOTS - 1))
            weights = jnp.exp2((s_ref[head % AHEAD_SLOTS, :count, :] - top) * RATE)
            both = jnp.dot(vflip, weights.astype(jnp.bfloat16), preferred_element_type=jnp.float32)
            summed, total = both[:HEAD_DIM, :], both[HEAD_DIM : HEAD_DIM + 1, :]
            if not fresh:
                factor = jnp.exp2((before - top) * RATE)
                total = total + total_ref[head : head + 1, :] * factor
                summed = summed + acc_ref[head] * factor
            top_ref[head : head + 1, :] = top
            total_ref[head : head + 1, :] = total
            acc_ref[head] = summed

    attend([(row, col)], True)

    @pl.when(col > 0)
    def _():
        wait_whole(row, mate_sem.at[0])
        attend([(row, mate)], False)

    def relay_near(dist):
        near = straight(dist)

        @pl.when(needs(row, near))
        def _():
            up = has_up & needs(row + lanes, near)
            across = needs(other, near)
            across_late = across & jnp.logical_not(split(near)) if splits else across
            for p in range(PIECES):
                wait_part(near, p, in_sem.at[2 * dist - 1, p])

                @pl.when(up)
                def _():
                    to_up(near, p, dist).start()

                if has_other:

                    @pl.when(across_late if p >= late_from else across)
                    def _():
                        to_other(near, p, dist).start()

                to_mate(near, p, 2 * dist).start()

    def relay_far(dist):
        far = crossed(dist)

        @pl.when(needs(row, far))
        def _():
            for p in range(PIECES):
                wait_part(far, p, in_sem.at[2 * dist, p])
                if splits and p >= late_from:

                    @pl.when(far_up(far))
                    def _():
                        to_far_up(far, p, dist).start()

                to_mate(far, p, 2 * dist + 1).start()

        if splits:

            @pl.when((far > row) & far_up(far))
            def _():
                for p in range(late_from, PIECES):
                    wait_part(far, p, in_sem.at[2 * dist, p])
                    to_far_up(far, p, dist).start()

    def early(dist):
        return (lane == lanes - 1) & (level == dist + 1) & (dist >= 1)

    def drain_own():
        @pl.when(own_up)
        def _():
            wait_whole(row, up_send.at[0])

        if has_other:

            @pl.when(own_cross)
            def _():
                wait_whole(row, cross_send.at[0])

        if splits:

            @pl.when(split(row) & has_up)
            def _():
                wait_rows(row, cuts[late_from], cuts[-1], cross_send.at[0])

        @pl.when(own_mate)
        def _():
            wait_whole(row, mate_send.at[0])

    def drain(dist):
        near = straight(dist)

        @pl.when(needs(row, near))
        def _():
            @pl.when(has_up & needs(row + lanes, near))
            def _():
                wait_whole(near, up_send.at[dist % 2])

            if has_other:

                if splits:

                    @pl.when(needs(other, near) & split(near))
                    def _():
                        wait_rows(near, 0, cuts[late_from], cross_send.at[dist % 2])

                @pl.when(needs(other, near) & jnp.logical_not(split(near)) if splits else needs(other, near))
                def _():
                    wait_whole(near, cross_send.at[dist % 2])

            wait_whole(near, mate_send.at[2 * dist % 4])

        if has_other:
            far = crossed(dist - 1)

            @pl.when(needs(row, far))
            def _():
                wait_whole(far, mate_send.at[(2 * dist - 1) % 4])

            if splits:

                @pl.when(far_up(far))
                def _():
                    wait_rows(far, cuts[late_from], cuts[-1], far_send.at[0])

    @pl.loop(1, furthest + 2)
    def _(dist):
        near, far = straight(dist), crossed(dist - 1)
        has_near = needs(row, near)
        has_far = needs(row, far) if has_other else jnp.bool_(False)
        both = has_near & has_far
        @pl.when(jnp.logical_not(early(dist - 1)))
        def _():
            relay_near(dist)

        if has_other:
            relay_far(dist - 1)

        @pl.when(dist == 1)
        def _():
            drain_own()

        @pl.when(dist > 1)
        def _():
            drain(dist - 1)

        single = jnp.where(has_near, near, far)
        single_unit = jnp.where(has_near, 2 * dist, 2 * dist - 1)
        alone = has_near != has_far

        @pl.loop(0, 2)
        def _(half):
            which = jnp.where(half == 0, col, mate)

            @pl.when(both)
            def _():
                @pl.when(half == 1)
                def _():
                    wait_whole(near, mate_sem.at[2 * dist])
                    if has_other:
                        wait_whole(far, mate_sem.at[2 * dist - 1])

                attend([(near, which), (far, which)], False)

            @pl.when((half == 0) & early(dist))
            def _():
                relay_near(dist + 1)

            @pl.when(alone)
            def _():
                @pl.when(half == 1)
                def _():
                    wait_whole(single, mate_sem.at[single_unit])

                attend([(single, which)], False)

    for head in range(heads):
        inverse = 1.0 / total_ref[head : head + 1, :]
        result = (acc_ref[head] * inverse).T
        o_ref[:, head * HEAD_DIM : (head + 1) * HEAD_DIM] = result.astype(o_ref.dtype)

    drain(furthest + 1)


def shards(n_row, n_col, queries, keys, values, doc_lengths):
    shard, width = queries.shape
    lanes = 2 if n_row % 2 == 0 else 1
    span = shard * n_row * n_col
    longest = (3 * span) // 4
    reach = min(n_row - 1, -(-longest // (shard * n_col)))
    levels = n_row // lanes
    furthest = min(levels - 1, (reach + lanes - 1) // lanes)
    heads = width // HEAD_DIM
    vmem = pl.BlockSpec(memory_space=pltpu.VMEM)
    whole = pl.BlockSpec(memory_space=pltpu.HBM)
    units = 2 * furthest + 2
    return pl.pallas_call(
        functools.partial(kernel, n_row, n_col, lanes, reach),
        out_shape=jax.ShapeDtypeStruct(queries.shape, queries.dtype),
        in_specs=[whole, whole, whole, whole],
        out_specs=vmem,
        scratch_shapes=[
            pltpu.SMEM(doc_lengths.shape, doc_lengths.dtype),
            pltpu.VMEM((n_row, n_col, 2 * shard, HEAD_DIM), keys.dtype),
            pltpu.VMEM((shard, width), queries.dtype),
            pltpu.VMEM((shard, HEAD_DIM), queries.dtype),
            pltpu.VMEM((heads, shard), jnp.float32),
            pltpu.VMEM((heads, shard), jnp.float32),
            pltpu.VMEM((heads, HEAD_DIM, shard), jnp.float32),
            pltpu.VMEM((AHEAD_SLOTS, n_col * shard, shard), jnp.float32),
            pltpu.SemaphoreType.DMA((3,)),
            pltpu.SemaphoreType.DMA((units - 1, PIECES)),
            pltpu.SemaphoreType.DMA((units,)),
            pltpu.SemaphoreType.DMA((2,)),
            pltpu.SemaphoreType.DMA((2,)),
            pltpu.SemaphoreType.DMA((4,)),
            pltpu.SemaphoreType.DMA((1,)),
        ],
        compiler_params=pltpu.CompilerParams(
            collective_id=0, has_side_effects=True, vmem_limit_bytes=24 << 20
        ),
        name="attend",
    )(*(pltpu.with_memory_space_constraint(x, pltpu.HBM) for x in (doc_lengths, queries, keys, values)))


def solution(mesh):
    placed = P(("groups", "row", "col"), None)
    return jax.shard_map(
        functools.partial(shards, mesh.shape["row"], mesh.shape["col"]),
        mesh=mesh,
        in_specs=(placed, placed, placed, P("groups")),
        out_specs=placed,
        check_vma=False,
    )
```

```python
import functools

import jax
import jax.numpy as jnp
from jax import lax
from jax.experimental import pallas as pl
from jax.experimental.pallas import tpu as pltpu
from jax.sharding import PartitionSpec as P

HEAD_DIM = 128
RATE = HEAD_DIM ** (-0.5) * 1.4426950408889634
MASKED = -1e30
AHEAD_SLOTS = 7
SUM_ROWS = 16
CUTS = (0, 5, 8)
PIECES = len(CUTS) - 1


def kernel(
    n_row,
    n_col,
    lanes,
    reach,
    lens_hbm,
    q_hbm,
    k_hbm,
    v_hbm,
    o_ref,
    lens_ref,
    kv,
    q_ref,
    member_ref,
    top_ref,
    total_ref,
    acc_ref,
    s_ref,
    load_sem,
    in_sem,
    mate_sem,
    up_send,
    cross_send,
    mate_send,
    far_send,
):
    shard = q_hbm.shape[0]
    heads = q_hbm.shape[1] // HEAD_DIM
    levels = n_row // lanes
    tile = n_col * shard
    cuts = [2 * shard * cut // CUTS[-1] for cut in CUTS]
    furthest = min(levels - 1, (reach + lanes - 1) // lanes)
    has_other = lanes > 1
    row = lax.axis_index("row")
    col = lax.axis_index("col")
    level = row // lanes
    lane = row % lanes
    mate = 1 - col
    other = level * lanes + (lanes - 1 - lane)
    has_up = level + 1 < levels
    has_down = level > 0

    def needs(reader, source):
        return (source >= 0) & (reader > source) & (reader - source <= reach)

    def straight(dist):
        return row - dist * lanes

    def crossed(dist):
        return other - dist * lanes

    barrier = pltpu.get_barrier_semaphore()
    pl.semaphore_signal(barrier, inc=1, device_id={"col": mate})
    if has_other:
        pl.semaphore_signal(barrier, inc=1, device_id={"row": other})

    @pl.when(has_up)
    def _():
        pl.semaphore_signal(barrier, inc=1, device_id={"row": row + lanes})

    @pl.when(has_down)
    def _():
        pl.semaphore_signal(barrier, inc=1, device_id={"row": row - lanes})

    load_k = pltpu.make_async_copy(k_hbm, kv.at[row, col, :shard, :], load_sem.at[0])
    load_v = pltpu.make_async_copy(v_hbm, kv.at[row, col, shard:, :], load_sem.at[0])
    load_q = pltpu.make_async_copy(q_hbm, q_ref, load_sem.at[1])
    load_lens = pltpu.make_async_copy(lens_hbm, lens_ref, load_sem.at[2])
    for load in (load_k, load_v, load_q, load_lens):
        load.start()

    def copy(source, rows, send_sem, recv_sem, device):
        here = kv.at[source, col, rows, :]
        return pltpu.make_async_remote_copy(
            src_ref=here,
            dst_ref=here,
            send_sem=send_sem,
            recv_sem=recv_sem,
            device_id=device,
            device_id_type=pl.DeviceIdType.MESH,
        )

    def part(p):
        return pl.ds(cuts[p], cuts[p + 1] - cuts[p])

    def to_up(source, p, dist):
        recv = in_sem.at[2 * dist + 1, p]
        return copy(source, part(p), up_send.at[dist % 2], recv, {"row": row + lanes})

    def to_other(source, p, dist):
        recv = in_sem.at[2 * dist, p]
        return copy(source, part(p), cross_send.at[dist % 2], recv, {"row": other})

    split_level = levels - 3
    late_from = PIECES // 2
    splits = has_other and split_level >= 0

    def split(source):
        return source == split_level * lanes + lanes - 1

    def far_up(source):
        return split(source) & has_up & needs(row + lanes, source)

    def to_far_up(source, p, dist):
        recv = in_sem.at[2 * dist + 2, p]
        return copy(source, part(p), far_send.at[0], recv, {"row": row + lanes})

    def wait_rows(source, start, stop, sem):
        here = kv.at[source, col, start:stop, :]
        pltpu.make_async_copy(here, here, sem).wait()

    def to_mate(source, p, unit):
        return copy(source, part(p), mate_send.at[unit % 4], mate_sem.at[unit], {"col": mate})

    def wait_whole(source, sem):
        here = kv.at[source, col, :, :]
        pltpu.make_async_copy(here, here, sem).wait()

    def wait_part(source, p, sem):
        here = kv.at[source, col, part(p), :]
        pltpu.make_async_copy(here, here, sem).wait()

    own_up = has_up
    own_cross = needs(other, row)
    own_mate = col < mate

    count = 1 + int(has_other) + has_up.astype(jnp.int32) + has_down.astype(jnp.int32)
    pl.semaphore_wait(barrier, count)
    wait_whole(row, load_sem.at[0])

    @pl.when(own_up)
    def _():
        for p in range(PIECES):
            to_up(row, p, 0).start()

    if has_other:

        @pl.when(own_cross)
        def _():
            for p in range(PIECES):
                to_other(row, p, 0).start()

    if splits:

        @pl.when(split(row) & has_up)
        def _():
            for p in range(late_from, PIECES):
                to_other(row, p, 0).start()

    @pl.when(own_mate)
    def _():
        for p in range(PIECES):
            to_mate(row, p, 0).start()

    first = (row * n_col + col) * shard
    qpos = first + lax.broadcasted_iota(jnp.int32, (1, shard), 1)

    def within(places):
        return (places >= begins) & (places < ends)

    lanes_of = lax.broadcasted_iota(jnp.int32, (1, HEAD_DIM), 1)
    begins = jnp.zeros((1, HEAD_DIM), jnp.int32)
    ends = jnp.full((1, HEAD_DIM), n_row * n_col * shard, jnp.int32)
    end = jnp.int32(0)
    load_lens.wait()
    docs = lens_ref.shape[0]
    for doc in range(docs):
        begins = jnp.where(lanes_of == doc, end, begins)
        end = end + lens_ref[doc]
        ends = jnp.where(lanes_of == doc, end, ends)
    offsets = lax.broadcasted_iota(jnp.int32, (shard, HEAD_DIM), 0)
    member = within(first + offsets) & (lanes_of < docs)
    member_ref[...] = jnp.where(member, 1.0, 0.0).astype(jnp.bfloat16)
    load_q.wait()

    def attend(blocks, fresh):
        count = shard * len(blocks)
        keys = jnp.concatenate([kv[at, which, :shard, :] for at, which in blocks], axis=0)
        vals = jnp.concatenate([kv[at, which, shard:, :] for at, which in blocks], axis=0)
        places = [at * tile + which * shard + offsets for at, which in blocks]
        apart = [jnp.where(within(place), 0.0, MASKED).astype(jnp.bfloat16) for place in places]
        kwide = jnp.concatenate([keys, jnp.concatenate(apart, axis=0)], axis=1)
        if fresh:
            kpos = first + lax.broadcasted_iota(jnp.int32, (count, shard), 0)
            bias = jnp.where(kpos <= qpos, jnp.float32(0.0), jnp.float32(MASKED))
        vflip = jnp.concatenate([vals.T, jnp.ones((SUM_ROWS, count), vals.dtype)], axis=0)

        def score(head):
            q = q_ref[:, head * HEAD_DIM : (head + 1) * HEAD_DIM]
            qwide = jnp.concatenate([q, member_ref[...]], axis=1)
            scores = lax.dot_general(
                kwide, qwide, (((1,), (1,)), ((), ())), preferred_element_type=jnp.float32
            )
            if fresh:
                scores = scores + bias
            s_ref[head % AHEAD_SLOTS, :count, :] = scores
            top = jnp.max(scores, axis=0, keepdims=True)
            if fresh:
                return top, top
            before = top_ref[head : head + 1, :]
            return before, jnp.maximum(before, top)

        tops = [score(head) for head in range(AHEAD_SLOTS - 1)]
        for head in range(heads):
            before, top = tops[head]
            if head + AHEAD_SLOTS - 1 < heads:
                tops.append(score(head + AHEAD_SLOTS - 1))
            weights = jnp.exp2((s_ref[head % AHEAD_SLOTS, :count, :] - top) * RATE)
            both = jnp.dot(vflip, weights.astype(jnp.bfloat16), preferred_element_type=jnp.float32)
            summed, total = both[:HEAD_DIM, :], both[HEAD_DIM : HEAD_DIM + 1, :]
            if not fresh:
                factor = jnp.exp2((before - top) * RATE)
                total = total + total_ref[head : head + 1, :] * factor
                summed = summed + acc_ref[head] * factor
            top_ref[head : head + 1, :] = top
            total_ref[head : head + 1, :] = total
            acc_ref[head] = summed

    attend([(row, col)], True)

    @pl.when(col > 0)
    def _():
        wait_whole(row, mate_sem.at[0])
        attend([(row, mate)], False)

    def relay_near(dist):
        near = straight(dist)

        @pl.when(needs(row, near))
        def _():
            up = has_up & needs(row + lanes, near)
            across = needs(other, near)
            across_late = across & jnp.logical_not(split(near)) if splits else across
            for p in range(PIECES):
                wait_part(near, p, in_sem.at[2 * dist - 1, p])

                @pl.when(up)
                def _():
                    to_up(near, p, dist).start()

                if has_other:

                    @pl.when(across_late if p >= late_from else across)
                    def _():
                        to_other(near, p, dist).start()

                to_mate(near, p, 2 * dist).start()

    def relay_far(dist):
        far = crossed(dist)

        @pl.when(needs(row, far))
        def _():
            for p in range(PIECES):
                wait_part(far, p, in_sem.at[2 * dist, p])
                if splits and p >= late_from:

                    @pl.when(far_up(far))
                    def _():
                        to_far_up(far, p, dist).start()

                to_mate(far, p, 2 * dist + 1).start()

        if splits:

            @pl.when((far > row) & far_up(far))
            def _():
                for p in range(late_from, PIECES):
                    wait_part(far, p, in_sem.at[2 * dist, p])
                    to_far_up(far, p, dist).start()

    def early(dist):
        return (lane == lanes - 1) & (level == dist + 1) & (dist >= 1)

    def drain_own():
        @pl.when(own_up)
        def _():
            wait_whole(row, up_send.at[0])

        if has_other:

            @pl.when(own_cross)
            def _():
                wait_whole(row, cross_send.at[0])

        if splits:

            @pl.when(split(row) & has_up)
            def _():
                wait_rows(row, cuts[late_from], cuts[-1], cross_send.at[0])

        @pl.when(own_mate)
        def _():
            wait_whole(row, mate_send.at[0])

    def drain(dist):
        near = straight(dist)

        @pl.when(needs(row, near))
        def _():
            @pl.when(has_up & needs(row + lanes, near))
            def _():
                wait_whole(near, up_send.at[dist % 2])

            if has_other:

                if splits:

                    @pl.when(needs(other, near) & split(near))
                    def _():
                        wait_rows(near, 0, cuts[late_from], cross_send.at[dist % 2])

                @pl.when(needs(other, near) & jnp.logical_not(split(near)) if splits else needs(other, near))
                def _():
                    wait_whole(near, cross_send.at[dist % 2])

            wait_whole(near, mate_send.at[2 * dist % 4])

        if has_other:
            far = crossed(dist - 1)

            @pl.when(needs(row, far))
            def _():
                wait_whole(far, mate_send.at[(2 * dist - 1) % 4])

            if splits:

                @pl.when(far_up(far))
                def _():
                    wait_rows(far, cuts[late_from], cuts[-1], far_send.at[0])

    @pl.loop(1, furthest + 2)
    def _(dist):
        near, far = straight(dist), crossed(dist - 1)
        has_near = needs(row, near)
        has_far = needs(row, far) if has_other else jnp.bool_(False)
        both = has_near & has_far
        @pl.when(jnp.logical_not(early(dist - 1)))
        def _():
            relay_near(dist)

        if has_other:
            relay_far(dist - 1)

        @pl.when(dist == 1)
        def _():
            drain_own()

        @pl.when(dist > 1)
        def _():
            drain(dist - 1)

        single = jnp.where(has_near, near, far)
        single_unit = jnp.where(has_near, 2 * dist, 2 * dist - 1)
        alone = has_near != has_far

        @pl.loop(0, 2)
        def _(half):
            which = jnp.where(half == 0, col, mate)

            @pl.when(both)
            def _():
                @pl.when(half == 1)
                def _():
                    wait_whole(near, mate_sem.at[2 * dist])
                    if has_other:
                        wait_whole(far, mate_sem.at[2 * dist - 1])

                attend([(near, which), (far, which)], False)

            @pl.when((half == 0) & early(dist))
            def _():
                relay_near(dist + 1)

            @pl.when(alone)
            def _():
                @pl.when(half == 1)
                def _():
                    wait_whole(single, mate_sem.at[single_unit])

                attend([(single, which)], False)

    for head in range(heads):
        inverse = 1.0 / total_ref[head : head + 1, :]
        result = (acc_ref[head] * inverse).T
        o_ref[:, head * HEAD_DIM : (head + 1) * HEAD_DIM] = result.astype(o_ref.dtype)

    drain(furthest + 1)


def shards(n_row, n_col, queries, keys, values, doc_lengths):
    shard, width = queries.shape
    lanes = 2 if n_row % 2 == 0 else 1
    span = shard * n_row * n_col
    longest = (3 * span) // 4
    reach = min(n_row - 1, -(-longest // (shard * n_col)))
    levels = n_row // lanes
    furthest = min(levels - 1, (reach + lanes - 1) // lanes)
    heads = width // HEAD_DIM
    vmem = pl.BlockSpec(memory_space=pltpu.VMEM)
    whole = pl.BlockSpec(memory_space=pltpu.HBM)
    units = 2 * furthest + 2
    return pl.pallas_call(
        functools.partial(kernel, n_row, n_col, lanes, reach),
        out_shape=jax.ShapeDtypeStruct(queries.shape, queries.dtype),
        in_specs=[whole, whole, whole, whole],
        out_specs=vmem,
        scratch_shapes=[
            pltpu.SMEM(doc_lengths.shape, doc_lengths.dtype),
            pltpu.VMEM((n_row, n_col, 2 * shard, HEAD_DIM), keys.dtype),
            pltpu.VMEM((shard, width), queries.dtype),
            pltpu.VMEM((shard, HEAD_DIM), queries.dtype),
            pltpu.VMEM((heads, shard), jnp.float32),
            pltpu.VMEM((heads, shard), jnp.float32),
            pltpu.VMEM((heads, HEAD_DIM, shard), jnp.float32),
            pltpu.VMEM((AHEAD_SLOTS, n_col * shard, shard), jnp.float32),
            pltpu.SemaphoreType.DMA((3,)),
            pltpu.SemaphoreType.DMA((units - 1, PIECES)),
            pltpu.SemaphoreType.DMA((units,)),
            pltpu.SemaphoreType.DMA((2,)),
            pltpu.SemaphoreType.DMA((2,)),
            pltpu.SemaphoreType.DMA((4,)),
            pltpu.SemaphoreType.DMA((1,)),
        ],
        compiler_params=pltpu.CompilerParams(
            collective_id=0, has_side_effects=True, vmem_limit_bytes=24 << 20
        ),
        name="attend",
    )(*(pltpu.with_memory_space_constraint(x, pltpu.HBM) for x in (doc_lengths, queries, keys, values)))


def solution(mesh):
    placed = P(("groups", "row", "col"), None)
    return jax.shard_map(
        functools.partial(shards, mesh.shape["row"], mesh.shape["col"]),
        mesh=mesh,
        in_specs=(placed, placed, placed, P("groups")),
        out_specs=placed,
        check_vma=False,
    )
```
